32 devices in a mesh: fsdp: 8 (over z, core), ctx: 4 (over y, x).
Axes of the slice: x: 2, y: 2, z: 4, core: 2. Of those that a mesh axis runs over, the one named last changes fastest.
Arguments:
- tokens: bfloat16 [8192, 2048], P(('fsdp', 'ctx')), may hold values from -6 to 6
- attn_gain: float32 [2048], replicated, may hold values from 0.5 to 1.5
- w_qkv: bfloat16 [2048, 4096], P('fsdp'), may hold values from -0.125 to 0.125
- q_gain: float32 [128], replicated, may hold values from 0.6 to 1.6, as said below
- k_gain: float32 [128], replicated, may hold values from 0.6 to 1.6, as said below
- w_out: bfloat16 [2048, 2048], P('fsdp'), may hold values from -1 to 1
- mlp_gain: float32 [2048], replicated, may hold values from 0.5 to 1.5
- w_gate_up: bfloat16 [2048, 12288], P('fsdp'), may hold values from -0.125 to 0.125
- w_down: bfloat16 [6144, 2048], P('fsdp'), may hold values from -0.078125 to 0.078125
- piece_order: int32 [8, 4], P('fsdp'), may hold values from 0 to 3, each once within a row
- cotangent: bfloat16 [8192, 2048], P(('fsdp', 'ctx')), may hold values from -6 to 6
Outputs:
- output: bfloat16 [8192, 2048], P(('fsdp', 'ctx'))
- d_tokens: float32 [8192, 2048], P(('fsdp', 'ctx'))
- d_attn_gain: float32 [2048], replicated
- d_w_qkv: float32 [2048, 4096], P('fsdp')
- d_q_gain: float32 [128], replicated
- d_k_gain: float32 [128], replicated
- d_w_out: float32 [2048, 2048], P('fsdp')
- d_mlp_gain: float32 [2048], replicated
- d_w_gate_up: float32 [2048, 12288], P('fsdp')
- d_w_down: float32 [6144, 2048], P('fsdp')
The draws below stay inside these ranges and needn't reach their ends.
Inputs may be any that keep to these rules, and one draw needn't show every extreme that they name: Each row is a permutation: the ctx index c of sequence s holds piece piece_order[s, c] of 256 tokens. `q_gain`: positive per-channel gains. `k_gain`: positive per-channel gains.
All inputs are finite; a program needn't handle non-finite values.
Results may differ from the reference program's by a relative error of at most 0.023.
Values may be sent and summed in bfloat16 or wider, within the bound.
No kernel may reach another device: no remote copies, remote signals or barrier semaphores. Data moves between devices by JAX's collectives and lax.ppermute only.
A program may use at most 448 MiB of HBM per device.

```python
import math
import jax
import jax.numpy as jnp
from jax import lax

D = 2048
HQ = 16
HK = 8
HD = 128
FF = 6144
PIECE = 256
SEQS = 8
TOKENS = 8192
N_FSDP = 8
N_CTX = 4


def gain_values(key):
    return jnp.exp(jax.random.uniform(key, (HD,), jnp.float32, math.log(0.6), math.log(1.6)))


def draw_q_gain(key, part):
    return gain_values(jax.random.fold_in(key, 11))


def draw_k_gain(key, part):
    return gain_values(jax.random.fold_in(key, 23))


def raised(array, stream_key, source, target, blocks, factor):
    def block_of(dim):
        return (jnp.arange(array.shape[dim]) // (array.shape[dim] // blocks)).reshape((-1,) + (1,) * (array.ndim - 1 - dim))

    one_side = jax.random.permutation(stream_key, blocks)[block_of(target)]
    second = (block_of(target) + blocks // 2) % blocks
    return jnp.where((block_of(source) == one_side) | (block_of(source) == second), factor * array, array)


def block_levels(stream_key, dims, shards, least, high):
    loudness = 1.0
    for dim, shards_of in shards:
        draws = jax.random.uniform(jax.random.fold_in(jax.random.fold_in(stream_key, 6), dim), (shards_of,), jnp.float32, least / len(shards), high / len(shards))
        loudness = loudness * jnp.repeat(jnp.exp(draws), dims[dim] // shards_of).reshape((-1,) + (1,) * (len(dims) - 1 - dim))
    return loudness


def gaussian(stream_key, dims, width, reach, pieces=(), kind=jnp.bfloat16):
    entries = jax.random.normal(stream_key, dims, jnp.float32) * width
    if len(pieces) > 0:
        entries = block_levels(stream_key, dims, pieces, -0.22, 0.18) * entries
    return jnp.clip(entries, min=-reach, max=reach).astype(kind)


def heavy_noise(own_key, dims, scale, most, pieces, heavy, kind=jnp.bfloat16):
    values = scale * jax.random.normal(own_key, dims, jnp.float32)
    if pieces:
        values = values * block_levels(own_key, dims, pieces, -0.22, 0.18)
    return jnp.clip(raised(values, jax.random.fold_in(own_key, 3), *heavy), -most, most).astype(kind)


def setup_inputs(seed: int = 0) -> dict:
    arg_keys = jax.random.split(jax.random.key(seed), 12)
    tokens = gaussian(arg_keys[0], (TOKENS, D), 1.0, 6.0, ((0, 32),))
    attn_gain = jnp.clip(1.0 + 0.1 * jax.random.normal(arg_keys[1], (D,), jnp.float32), 0.5, 1.5)
    w_qkv = gaussian(arg_keys[2], (D, (HQ + 2 * HK) * HD), D ** -0.5, 0.125, ((0, 8),))
    q_gain = draw_q_gain(jax.random.fold_in(arg_keys[11], 71), 0)
    k_gain = draw_k_gain(jax.random.fold_in(arg_keys[11], 71), 0)
    w_out = gaussian(arg_keys[5], (HQ * HD, D), (HQ * HD // 64) ** -0.5, 1.0, ((0, 8),))
    mlp_gain = jnp.clip(1.0 + 0.1 * jax.random.normal(arg_keys[6], (D,), jnp.float32), 0.5, 1.5)
    w_gate_up = gaussian(arg_keys[7], (D, 2 * FF), D ** -0.5, 0.125, ((0, 8),))
    w_down = gaussian(arg_keys[8], (FF, D), FF ** -0.5, 0.078125, ((0, 8),))
    piece_order = jax.vmap(lambda own: jax.random.permutation(own, N_CTX))(jax.random.split(arg_keys[9], SEQS)).reshape((SEQS, N_CTX)).astype(jnp.int32)
    cotangent = heavy_noise(arg_keys[10], (TOKENS, D), 1.0, 6.0, ((0, 32),), (0, 1, 32, 2.75))
    return {"tokens": tokens, "attn_gain": attn_gain, "w_qkv": w_qkv, "q_gain": q_gain, "k_gain": k_gain, "w_out": w_out, "mlp_gain": mlp_gain, "w_gate_up": w_gate_up, "w_down": w_down, "piece_order": piece_order, "cotangent": cotangent}


EPS = 1e-06
THETA = 1000000.0

@jax.custom_vjp
def low(v):
    return lax.optimization_barrier(v.astype(jnp.bfloat16)).astype(jnp.float32)

@jax.custom_vjp
def low_back(v):
    return v

def low_keep(v):
    return (low(v), None)

def low_pass(kept, grad):
    return (grad,)

def back_keep(v):
    return (v, None)

def back_low(kept, grad):
    return (low(grad),)
low.defvjp(low_keep, low_pass)
low_back.defvjp(back_keep, back_low)

def norm_scale(tensor, gain_vec):
    return tensor * lax.rsqrt(lax.optimization_barrier(jnp.mean(tensor * tensor, axis=-1, keepdims=True)) + EPS) * gain_vec

def frequencies():
    return THETA ** (-(jnp.arange(HD // 2, dtype=jnp.float32) * 2.0) / HD)

def rotate(tensor, angles):
    half_dim = tensor.shape[-1] // 2
    cosine = jnp.cos(angles)[:, None, :]
    sine_part = jnp.sin(angles)[:, None, :]
    front_half = tensor[..., :half_dim]
    back_half = tensor[..., half_dim:]
    return jnp.concatenate([front_half * cosine - back_half * sine_part, back_half * cosine + front_half * sine_part], axis=-1)

def head_part(projected, q_gain, k_gain, angles):
    tok_rows = projected.shape[0]
    queries = projected[:, :HQ * HD].reshape(tok_rows, HQ, HD)
    key_heads = projected[:, HQ * HD:(HQ + HK) * HD].reshape(tok_rows, HK, HD)
    queries = rotate(norm_scale(queries, q_gain), angles)
    key_heads = rotate(norm_scale(key_heads, k_gain), angles)
    return (queries.reshape(tok_rows, HQ * HD), key_heads.reshape(tok_rows, HK * HD))

def reference(tokens, attn_gain, w_qkv, q_gain, k_gain, w_out, mlp_gain, w_gate_up, w_down, piece_order, cotangent):
    seq_len = PIECE * N_CTX
    q_block = min(512, seq_len)
    group_size = HQ // HK
    highest = lax.Precision.HIGHEST
    score_scale = HD ** (-0.5)
    positions = (piece_order[:, :, None] * PIECE + jnp.arange(PIECE, dtype=jnp.int32)[None, None, :]).reshape(N_FSDP, seq_len).astype(jnp.int32)

    def forward(inputs, attn_gain, w_qkv, q_gain, k_gain, w_out, mlp_gain, w_gate_up, w_down):

        def one_sequence(seq_args):
            seq_rows, seq_pos = seq_args
            normed = low(norm_scale(seq_rows, attn_gain))
            projected = low_back(jnp.dot(normed, w_qkv, precision=highest, preferred_element_type=jnp.float32))
            angles = seq_pos.astype(jnp.float32)[:, None] * frequencies()[None, :]
            q_flat, k_flat = head_part(projected, q_gain, k_gain, angles)
            queries = low_back(low(q_flat)).reshape(seq_len, HK, group_size, HD)
            key_heads = low_back(low(k_flat)).reshape(seq_len, HK, HD)
            values = low_back(low(projected[:, (HQ + HK) * HD:])).reshape(seq_len, HK, HD)

            def attend(pair):
                query_part, query_pos = pair
                scores = low_back(jnp.einsum('qkgd,rkd->kgqr', query_part, key_heads, precision=highest) * score_scale)
                allowed = seq_pos[None, :] <= query_pos[:, None]
                scores = jnp.where(allowed, scores, -1e+30)
                prob_block = low(jax.nn.softmax(scores, axis=-1))
                mixed_heads = jnp.einsum('kgqr,rkd->qkgd', prob_block, values, precision=highest)
                return mixed_heads.reshape(q_block, HQ * HD)
            query_blocks = queries.reshape(seq_len // q_block, q_block, HK, group_size, HD)
            pos_blocks = seq_pos.reshape(seq_len // q_block, q_block)
            attn = lax.map(jax.checkpoint(attend), (query_blocks, pos_blocks)).reshape(seq_len, HQ * HD)
            attn = low(low_back(attn))
            branch = low_back(jnp.dot(attn, w_out, precision=highest, preferred_element_type=jnp.float32))
            residual = seq_rows + branch
            mlp_in = low(norm_scale(residual, mlp_gain))
            gate_up = low_back(jnp.dot(mlp_in, w_gate_up, precision=highest, preferred_element_type=jnp.float32))
            swiglu_out = low(jax.nn.silu(gate_up[:, :FF]) * gate_up[:, FF:])
            return residual + low_back(jnp.dot(swiglu_out, w_down, precision=highest, preferred_element_type=jnp.float32))
        stacked = lax.map(jax.checkpoint(one_sequence), (inputs.reshape(N_FSDP, seq_len, D), positions))
        return stacked.reshape(TOKENS, D)
    floats = (tokens.astype(jnp.float32), attn_gain, w_qkv.astype(jnp.float32), q_gain, k_gain, w_out.astype(jnp.float32), mlp_gain, w_gate_up.astype(jnp.float32), w_down.astype(jnp.float32))
    output, backward = jax.vjp(forward, *floats)
    grad_list = backward(cotangent.astype(jnp.float32))
    return (output.astype(jnp.bfloat16), grad_list[0], grad_list[1], grad_list[2], grad_list[3], grad_list[4], grad_list[5], grad_list[6], grad_list[7], grad_list[8])
```

```python
import functools

import jax
import jax.numpy as jnp
from jax import lax
from jax.experimental import pallas as pl
from jax.experimental.pallas import tpu as pltpu
from jax.sharding import PartitionSpec as P

HQ = 16
HK = 8
HD = 128
FF = 6144
GROUP = HQ // HK


EPS = 1e-06
THETA = 1000000.0
BF = jnp.bfloat16
F32 = jnp.float32


def norm_scale(tensor, gain_vec):
    return tensor * lax.rsqrt(jnp.mean(tensor * tensor, axis=-1, keepdims=True) + EPS) * gain_vec


def frequencies():
    return THETA ** (-(jnp.arange(HD // 2, dtype=jnp.float32) * 2.0) / HD)


def rotate(tensor, angles):
    half_dim = tensor.shape[-1] // 2
    cosine = jnp.cos(angles)[:, None, :]
    sine_part = jnp.sin(angles)[:, None, :]
    front_half = tensor[..., :half_dim]
    back_half = tensor[..., half_dim:]
    return jnp.concatenate(
        [front_half * cosine - back_half * sine_part, back_half * cosine + front_half * sine_part],
        axis=-1,
    )


def head_part(projected, q_gain, k_gain, angles, hq, hk):
    rows = projected.shape[0]
    queries = projected[:, : hq * HD].reshape(rows, hq, HD)
    key_heads = projected[:, hq * HD :].reshape(rows, hk, HD)
    queries = rotate(norm_scale(queries, q_gain), angles)
    key_heads = rotate(norm_scale(key_heads, k_gain), angles)
    return (queries.reshape(rows, hq * HD), key_heads.reshape(rows, hk * HD))


def dot(a, b):
    return jnp.dot(a, b, preferred_element_type=F32)


def dot_t(a, b):
    return lax.dot_general(a, b, (((1,), (1,)), ((), ())), preferred_element_type=F32)


def tdot(a, b):
    return lax.dot_general(a, b, (((0,), (0,)), ((), ())), preferred_element_type=F32)


class Ctx:
    def __init__(self):
        self.size = lax.axis_size("ctx")
        self.me = lax.axis_index("ctx")
        self.paired = self.size == 4
        if self.paired:
            self.order = [self.me ^ i for i in range(4)]
        else:
            self.order = list(range(self.size))

    def hop(self, value, bit):
        return lax.ppermute(value, "ctx", [(i, i ^ bit) for i in range(self.size)])

    def gather(self, value):
        if not self.paired:
            whole = lax.all_gather(value, "ctx", axis=0)
            return [whole[i] for i in range(self.size)]
        half = value.shape[0] // 2
        from_x = self.hop(value, 1)
        from_y = self.hop(value, 2)
        low = self.hop(from_y[:half], 1)
        high = self.hop(from_x[half:], 2)
        return [value, from_x, from_y, jnp.concatenate([low, high], axis=0)]

    def scatter_sum(self, parts):
        if not self.paired:
            whole = jnp.concatenate([p.astype(BF) for p in parts], axis=0)
            return lax.psum_scatter(whole, "ctx", scatter_dimension=0, tiled=True).astype(F32)
        half = parts[0].shape[0] // 2
        far = parts[3].astype(BF)
        low = self.hop(far[:half], 1).astype(F32)
        high = self.hop(far[half:], 2).astype(F32)
        to_x = jnp.concatenate([parts[1][:half], parts[1][half:] + high], axis=0).astype(BF)
        to_y = jnp.concatenate([parts[2][:half] + low, parts[2][half:]], axis=0).astype(BF)
        return parts[0] + self.hop(to_x, 1).astype(F32) + self.hop(to_y, 2).astype(F32)

    def exchange(self, blocks):
        if not self.paired:
            return lax.all_to_all(blocks, "ctx", 0, 0, tiled=True)
        out = jnp.zeros_like(blocks)
        for i in range(4):
            there = self.order[i]
            block = lax.dynamic_index_in_dim(blocks, there, 0, keepdims=True)
            if i:
                block = self.hop(block, i)
            out = lax.dynamic_update_slice_in_dim(out, block, there, 0)
        return out

    def in_order(self, blocks):
        if not self.paired:
            return blocks
        return [lax.select_n(self.me ^ j, *blocks) for j in range(4)]


def pick_kernel(groups, stride, part, size, me_ref, in_ref, out_ref):
    for c in range(size):

        @pl.when(me_ref[0] == c)
        def _():
            out_ref[...] = jnp.concatenate(
                [in_ref[:, g * stride + c * part : g * stride + (c + 1) * part] for g in range(groups)],
                axis=1,
            )


def pick_columns(weight, me, size, groups):
    rows, width = weight.shape
    stride = width // groups
    part = stride // size
    step = 64
    return pl.pallas_call(
        functools.partial(pick_kernel, groups, stride, part, size),
        grid_spec=pltpu.PrefetchScalarGridSpec(
            num_scalar_prefetch=1,
            grid=(rows // step,),
            in_specs=[pl.BlockSpec((step, width), lambda i, me: (i, 0))],
            out_specs=pl.BlockSpec((step, groups * part), lambda i, me: (i, 0)),
        ),
        out_shape=jax.ShapeDtypeStruct((rows, groups * part), weight.dtype),
        cost_estimate=pl.CostEstimate(flops=0, bytes_accessed=4 * weight.size, transcendentals=0),
        name="pick_columns",
    )(me.reshape(1), weight)


def spread_kernel(groups, part, paired, me_ref, *refs):
    ins, out_ref = refs[:-1], refs[-1]
    size = len(ins)
    stride = part * size

    def write(order):
        for g in range(groups):
            out_ref[:, g * stride : (g + 1) * stride] = jnp.concatenate(
                [ins[order[j]][:, g * part : (g + 1) * part].astype(F32) for j in range(size)], axis=1
            )

    if not paired:
        write(list(range(size)))
        return
    for c in range(size):

        @pl.when(me_ref[0] == c)
        def _():
            write([c ^ j for j in range(size)])


def spread_columns(blocks, me, paired, groups):
    rows, width = blocks[0].shape
    part = width // groups
    size = len(blocks)
    step = 32
    return pl.pallas_call(
        functools.partial(spread_kernel, groups, part, paired),
        grid_spec=pltpu.PrefetchScalarGridSpec(
            num_scalar_prefetch=1,
            grid=(rows // step,),
            in_specs=[pl.BlockSpec((step, width), lambda i, me: (i, 0))] * size,
            out_specs=pl.BlockSpec((step, width * size), lambda i, me: (i, 0)),
        ),
        out_shape=jax.ShapeDtypeStruct((rows, width * size), F32),
        cost_estimate=pl.CostEstimate(
            flops=0, bytes_accessed=6 * rows * width * size, transcendentals=0
        ),
        name="spread_columns",
    )(me.reshape(1), *blocks)


def gather_rows(weight):
    return lax.all_gather(weight, "fsdp", axis=0, tiled=True)


def scatter_rows(grad):
    return lax.psum_scatter(grad.astype(BF), "fsdp", scatter_dimension=0, tiled=True)


def shards(
    tokens,
    attn_gain,
    w_qkv,
    q_gain,
    k_gain,
    w_out,
    mlp_gain,
    w_gate_up,
    w_down,
    piece_order,
    cotangent,
):
    rows, width = tokens.shape
    ctx = Ctx()
    nc, me = ctx.size, ctx.me
    nf = lax.axis_size("fsdp")
    hq, hk = HQ // nc, HK // nc
    pieces = piece_order[0]
    score_scale = HD ** (-0.5)
    total = nc * rows
    ff = FF // nc

    def cols(weight, start, count):
        return lax.dynamic_slice_in_dim(weight, start + me * count, count, axis=1)

    qkv_mine = jnp.concatenate(
        [
            cols(w_qkv, 0, hq * HD),
            cols(w_qkv, HQ * HD, hk * HD),
            cols(w_qkv, (HQ + HK) * HD, hk * HD),
        ],
        axis=1,
    )
    with jax.named_scope("w_qkv"):
        qkv = gather_rows(qkv_mine)
    with jax.named_scope("w_out"):
        out_cols = gather_rows(cols(w_out, 0, width // nc))
    with jax.named_scope("w_gate_up"):
        gu_mine = pick_columns(w_gate_up, me, nc, 2 * nf)
        gu = gather_rows(gu_mine)
    with jax.named_scope("w_down"):
        part = w_down.shape[0] // nc
        down = gather_rows(lax.dynamic_slice_in_dim(w_down, me * part, part, axis=0))

    with jax.named_scope("tok_gather"):
        token_rows = jnp.concatenate(ctx.gather(tokens), axis=0)
    positions = jnp.concatenate(
        [
            lax.dynamic_index_in_dim(pieces, there, 0) * rows + jnp.arange(rows, dtype=jnp.int32)
            for there in ctx.order
        ]
    )
    angles = positions.astype(F32)[:, None] * frequencies()[None, :]
    normed = norm_scale(token_rows.astype(F32), attn_gain).astype(BF)

    with jax.named_scope("w_out_x"):
        out_blocks = ctx.exchange(out_cols.reshape(nc, hq * HD, width // nc))
        out_mine = jnp.concatenate([out_blocks[j] for j in range(nc)], axis=1)

    with jax.named_scope("qkv"):
        projected = dot(normed, qkv)
    qk_rows, head_back = jax.vjp(
        lambda p, gq, gk: head_part(p, gq, gk, angles, hq, hk),
        projected[:, : (hq + hk) * HD],
        q_gain,
        k_gain,
    )
    queries = qk_rows[0].astype(BF).reshape(total, hk, GROUP, HD)
    keys = qk_rows[1].astype(BF).reshape(total, hk, HD)
    values = projected[:, (hq + hk) * HD :].astype(BF).reshape(total, hk, HD)
    allowed = positions[None, :] <= positions[:, None]

    with jax.named_scope("attn"):
        scores = jnp.einsum("qkgd,rkd->kgqr", queries, keys, preferred_element_type=F32) * score_scale
        scores = jnp.where(allowed, scores, -1e30)
        top = jnp.max(scores, axis=-1)
        weights = jnp.exp(scores - top[..., None])
        weight_sum = jnp.sum(weights, axis=-1)
        acc = jnp.einsum("kgqr,rkd->kgqd", weights.astype(BF), values, preferred_element_type=F32)
        attn_heads = acc / weight_sum[..., None]
        log_total = top + jnp.log(weight_sum)
        attn_low = jnp.transpose(attn_heads, (2, 0, 1, 3)).reshape(total, hq * HD).astype(BF)

    with jax.named_scope("branch"):
        parts = [dot(attn_low[i * rows : (i + 1) * rows], out_mine) for i in range(nc)]
        branch = ctx.scatter_sum(parts)
    inputs = tokens.astype(F32)
    residual = inputs + branch
    mlp_f32, second_back = jax.vjp(norm_scale, residual, mlp_gain)
    with jax.named_scope("mlp_gather"):
        mlp_rows = jnp.concatenate(ctx.gather(mlp_f32.astype(BF)), axis=0)
    with jax.named_scope("cot_gather"):
        cot_rows = jnp.concatenate(ctx.gather(cotangent), axis=0)
    with jax.named_scope("gate_up"):
        gate_up = dot(mlp_rows, gu)
        gate, up = gate_up[:, :ff], gate_up[:, ff:]
        swiglu_f32, swiglu_back = jax.vjp(lambda g, u: jax.nn.silu(g) * u, gate, up)
        swiglu_out = swiglu_f32.astype(BF)
    with jax.named_scope("d_w_down"):
        grad_down = scatter_rows(tdot(swiglu_out, cot_rows))
    with jax.named_scope("d_swiglu"):
        grad_swiglu = dot_t(cot_rows, down)
        grad_gate, grad_up = swiglu_back(grad_swiglu)
        grad_gate_up = jnp.concatenate([grad_gate, grad_up], axis=1).astype(BF)
    with jax.named_scope("d_w_gate_up"):
        grad_gu = scatter_rows(tdot(mlp_rows, grad_gate_up))
    with jax.named_scope("d_mlp_in"):
        parts = [dot_t(grad_gate_up[i * rows : (i + 1) * rows], gu) for i in range(nc)]
        grad_mlp_in = ctx.scatter_sum(parts)
    with jax.named_scope("down"):
        parts = [dot(swiglu_out[i * rows : (i + 1) * rows], down) for i in range(nc)]
        output = (residual + ctx.scatter_sum(parts)).astype(BF)
    grad_norm_mlp, grad_mlp_gain = second_back(grad_mlp_in)
    grad_residual = cotangent.astype(F32) + grad_norm_mlp
    with jax.named_scope("branch_gather"):
        branch_rows = jnp.concatenate(ctx.gather(grad_residual.astype(BF)), axis=0)
    with jax.named_scope("d_attn"):
        grad_attn = dot_t(branch_rows, out_mine).astype(BF)
    with jax.named_scope("d_w_out"):
        grad_out = tdot(attn_low, branch_rows).astype(BF)
        grad_out = jnp.stack(
            [grad_out[:, j * (width // nc) : (j + 1) * (width // nc)] for j in range(nc)]
        )
        grad_out = scatter_rows(ctx.exchange(grad_out).reshape(width, width // nc))
    with jax.named_scope("attn_back"):
        grad_heads = grad_attn.reshape(total, hk, GROUP, HD)
        row_delta = jnp.sum(
            attn_heads * jnp.transpose(grad_heads, (1, 2, 0, 3)).astype(F32), axis=-1
        )
        scores = jnp.einsum("qkgd,rkd->kgqr", queries, keys, preferred_element_type=F32) * score_scale
        probs = jnp.where(
            allowed, jnp.exp(jnp.where(allowed, scores, -1e30) - log_total[..., None]), 0.0
        )
        grad_probs = jnp.einsum("qkgd,rkd->kgqr", grad_heads, values, preferred_element_type=F32)
        grad_scores = (probs * (grad_probs - row_delta[..., None])).astype(BF)
        grad_query = score_scale * jnp.einsum(
            "kgqr,rkd->qkgd", grad_scores, keys, preferred_element_type=F32
        )
        grad_keys = score_scale * jnp.einsum(
            "kgqr,qkgd->rkd", grad_scores, queries, preferred_element_type=F32
        )
        grad_values = jnp.einsum(
            "kgqr,qkgd->rkd", probs.astype(BF), grad_heads, preferred_element_type=F32
        )
    grad_qk, grad_q_gain, grad_k_gain = head_back(
        (grad_query.reshape(total, hq * HD), grad_keys.reshape(total, hk * HD))
    )
    grad_projected = jnp.concatenate(
        [grad_qk, grad_values.reshape(total, hk * HD)], axis=1
    ).astype(BF)
    with jax.named_scope("d_w_qkv"):
        grad_qkv = scatter_rows(tdot(normed, grad_projected))
    with jax.named_scope("d_normed"):
        parts = [dot_t(grad_projected[i * rows : (i + 1) * rows], qkv) for i in range(nc)]
        grad_normed = ctx.scatter_sum(parts)
    _, first_back = jax.vjp(norm_scale, inputs, attn_gain)
    grad_norm_in, grad_attn_gain = first_back(grad_normed)
    grad_tokens = grad_residual + grad_norm_in

    with jax.named_scope("g_down"):
        grad_down = jnp.concatenate(ctx.in_order(ctx.gather(grad_down)), axis=0).astype(F32)
    with jax.named_scope("g_gate_up"):
        grad_gu = spread_columns(ctx.gather(grad_gu), me, ctx.paired, 2 * nf)
    with jax.named_scope("g_out"):
        grad_out = jnp.concatenate(ctx.in_order(ctx.gather(grad_out)), axis=1).astype(F32)
    with jax.named_scope("g_qkv"):
        blocks = ctx.in_order(ctx.gather(grad_qkv))
        cuts = [(0, hq * HD), (hq * HD, (hq + hk) * HD), ((hq + hk) * HD, (hq + 2 * hk) * HD)]
        grad_qkv = jnp.concatenate([b[:, lo:hi] for lo, hi in cuts for b in blocks], axis=1)
        grad_qkv = grad_qkv.astype(F32)
    gain_grads = lax.psum(
        (grad_attn_gain, grad_mlp_gain, grad_q_gain, grad_k_gain), ("fsdp", "ctx")
    )
    return (
        output,
        grad_tokens,
        gain_grads[0],
        grad_qkv,
        gain_grads[2],
        gain_grads[3],
        grad_out,
        gain_grads[1],
        grad_gu,
        grad_down,
    )


def solution(mesh):
    in_specs = (
        P(("fsdp", "ctx"), None),
        P(),
        P("fsdp", None),
        P(),
        P(),
        P("fsdp", None),
        P(),
        P("fsdp", None),
        P("fsdp", None),
        P("fsdp", None),
        P(("fsdp", "ctx"), None),
    )
    out_specs = (
        P(("fsdp", "ctx"), None),
        P(("fsdp", "ctx"), None),
        P(),
        P("fsdp", None),
        P(),
        P(),
        P("fsdp", None),
        P(),
        P("fsdp", None),
        P("fsdp", None),
    )
    return jax.shard_map(shards, mesh=mesh, in_specs=in_specs, out_specs=out_specs, check_vma=False)
```
